32 devices in a mesh: shard: 4 (over y, x), context: 2 (over core), tensor: 4 (over z).
Axes of the slice: x: 2, y: 2, z: 4, core: 2. Of those that a mesh axis runs over, the one named last changes fastest.
Arguments:
- tokens: bfloat16 [8192, 640], P(('shard', 'context')), may hold values from -6 to 6
- query_weight: bfloat16 [640, 1024], P(('shard', 'context'), 'tensor'), may hold values from -0.25 to 0.25
- keyvalue_weight: bfloat16 [640, 512], P(('shard', 'context')), may hold values from -0.25 to 0.25
- output_weight: bfloat16 [640, 1024], P(('shard', 'context'), 'tensor'), may hold values from -0.1875 to 0.1875
- gate_weight: bfloat16 [640, 2048], P(('shard', 'context'), 'tensor'), may hold values from -0.25 to 0.25
- up_weight: bfloat16 [640, 2048], P(('shard', 'context'), 'tensor'), may hold values from -0.25 to 0.25
- down_weight: bfloat16 [640, 2048], P(('shard', 'context'), 'tensor'), may hold values from -0.125 to 0.125
- attn_in_gain: float32 [640], replicated, may hold values from 0.5 to 2
- attn_out_gain: float32 [640], replicated, may hold values from 0.5 to 2
- ffn_in_gain: float32 [640], replicated, may hold values from 0.5 to 2
- ffn_out_gain: float32 [640], replicated, may hold values from 0.5 to 2
- query_gain: float32 [256], replicated, may hold values from 0.5 to 2
- key_gain: float32 [256], replicated, may hold values from 0.5 to 2
- positions: int32 [8192], P(('shard', 'context')), may hold values from 0 to 2047, as said below
- cotangent: bfloat16 [8192, 640], P(('shard', 'context')), may hold values from -6 to 6
Outputs:
- mixed_out: bfloat16 [8192, 640], P(('shard', 'context'))
- input_grad: float32 [8192, 640], P(('shard', 'context'))
- query_grad: float32 [640, 1024], P(('shard', 'context'), 'tensor')
- keyvalue_grad: float32 [640, 512], P(('shard', 'context'))
- output_grad: float32 [640, 1024], P(('shard', 'context'), 'tensor')
- gate_grad: float32 [640, 2048], P(('shard', 'context'), 'tensor')
- up_grad: float32 [640, 2048], P(('shard', 'context'), 'tensor')
- down_grad: float32 [640, 2048], P(('shard', 'context'), 'tensor')
- attn_in_grad: float32 [640], P(('shard', 'context'))
- attn_out_grad: float32 [640], P(('shard', 'context'))
- ffn_in_grad: float32 [640], P(('shard', 'context'))
- ffn_out_grad: float32 [640], P(('shard', 'context'))
- query_gain_grad: float32 [256], P(('shard', 'context'))
- key_gain_grad: float32 [256], P(('shard', 'context'))
The draws below stay inside these ranges and needn't reach their ends.
Inputs may be any that keep to these rules, and one draw needn't show every extreme that they name: Each token of a device stands in the same sequence; a device's 1024 tokens have consecutive positions, and the positions of a sequence are a permutation of 0 to 2047.
All inputs are finite; a program needn't handle non-finite values.
Results may differ from the reference program's by a relative error of at most 0.018.
Values may be sent and summed in bfloat16 or wider, within the bound.
No kernel may reach another device: no remote copies, remote signals or barrier semaphores. Data moves between devices by JAX's collectives and lax.ppermute only.
A program may use at most 192 MiB of HBM per device.

```python
import math
import jax
import jax.numpy as jnp
from jax import lax

D = 640
HEADS = 4
HEAD = 256
FF = 2048
TOK_DEV = 1024
SEQS = 4
LENGTH = 2048
TOKENS = 8192


def head_gain(key, salt):
    return jnp.exp(jax.random.uniform(jax.random.fold_in(key, salt), (HEAD,), jnp.float32, math.log(0.5), math.log(2.0)))


def draw_query_gain(key, part):
    return head_gain(key, 1)


def draw_key_gain(key, part):
    return head_gain(key, 2)


def draw_positions(key, part):
    seq_keys = jax.random.split(jax.random.fold_in(key, 3), SEQS)
    order = jax.vmap(lambda one_key: jax.random.permutation(one_key, LENGTH // TOK_DEV))(seq_keys)
    steps_in = jnp.arange(TOK_DEV, dtype=jnp.int32)
    return (order.astype(jnp.int32)[:, :, None] * TOK_DEV + steps_in[None, None, :]).reshape(SEQS * LENGTH).astype(jnp.int32)


def block_scale(stream_key, extent, pieces, low, high):
    level, own = 1.0, jax.random.fold_in(stream_key, 6)
    for dim, blocks in pieces:
        draws = jnp.exp(jax.random.uniform(jax.random.fold_in(own, dim), (blocks,), jnp.float32, low / len(pieces), high / len(pieces)))
        level = level * jnp.repeat(draws, extent[dim] // blocks).reshape([-1 if axis == dim else 1 for axis in range(len(extent))])
    return level


def scatter_about(stream_key, dims, scale, bound, cuts=(), kind=jnp.bfloat16):
    level = block_scale(stream_key, dims, cuts, -0.22, 0.18) if cuts else 1.0
    values = jax.random.normal(stream_key, dims, jnp.float32) * scale * level
    return jnp.minimum(jnp.maximum(values, -bound), bound).astype(kind)


def setup_inputs(seed: int = 0) -> dict:
    key_list = jax.random.split(jax.random.key(seed), 16)
    tokens = scatter_about(key_list[0], (TOKENS, D), 1.0, 6.0, ((0, 8),))
    query_weight = scatter_about(key_list[1], (D, HEADS * HEAD), D ** -0.5, 0.25, ((0, 8), (1, 4)))
    keyvalue_weight = scatter_about(key_list[2], (D, 2 * HEAD), D ** -0.5, 0.25, ((0, 8),))
    output_weight = scatter_about(key_list[3], (D, HEADS * HEAD), (HEADS * HEAD) ** -0.5, 0.1875, ((0, 8), (1, 4)))
    gate_weight = scatter_about(key_list[4], (D, FF), D ** -0.5, 0.25, ((0, 8), (1, 4)))
    up_weight = scatter_about(key_list[5], (D, FF), D ** -0.5, 0.25, ((0, 8), (1, 4)))
    down_weight = scatter_about(key_list[6], (D, FF), FF ** -0.5, 0.125, ((0, 8), (1, 4)))
    attn_in_gain = jnp.clip(jnp.exp(jax.random.uniform(key_list[7], (D,), jnp.float32, math.log(0.5), math.log(2.0))), 0.5, 2.0)
    attn_out_gain = jnp.clip(jnp.exp(jax.random.uniform(key_list[8], (D,), jnp.float32, math.log(0.5), math.log(2.0))), 0.5, 2.0)
    ffn_in_gain = jnp.clip(jnp.exp(jax.random.uniform(key_list[9], (D,), jnp.float32, math.log(0.5), math.log(2.0))), 0.5, 2.0)
    ffn_out_gain = jnp.clip(jnp.exp(jax.random.uniform(key_list[10], (D,), jnp.float32, math.log(0.5), math.log(2.0))), 0.5, 2.0)
    query_gain = draw_query_gain(jax.random.fold_in(key_list[15], 71), 0)
    key_gain = draw_key_gain(jax.random.fold_in(key_list[15], 71), 0)
    positions = draw_positions(jax.random.fold_in(key_list[15], 71), 0)
    cotangent = scatter_about(key_list[14], (TOKENS, D), 1.0, 6.0, ((0, 8),))
    return dict(tokens=tokens, query_weight=query_weight, keyvalue_weight=keyvalue_weight, output_weight=output_weight, gate_weight=gate_weight, up_weight=up_weight, down_weight=down_weight, attn_in_gain=attn_in_gain, attn_out_gain=attn_out_gain, ffn_in_gain=ffn_in_gain, ffn_out_gain=ffn_out_gain, query_gain=query_gain, key_gain=key_gain, positions=positions, cotangent=cotangent)


EPS = 1e-06
HIGH = lax.Precision.HIGHEST

@jax.custom_vjp
def low(v):
    return lax.optimization_barrier(v.astype(jnp.bfloat16)).astype(jnp.float32)

@jax.custom_vjp
def low_back(v):
    return v

def low_keep(v):
    return (low(v), None)

def low_pass(kept, grad):
    return (grad,)

def back_keep(v):
    return (v, None)

def back_low(kept, grad):
    return (low(grad),)
low.defvjp(low_keep, low_pass)
low_back.defvjp(back_keep, back_low)

def unit_rows(values_in):
    return values_in * lax.rsqrt(lax.optimization_barrier(jnp.mean(values_in * values_in, axis=-1, keepdims=True)) + EPS)

def rotate(values_in, cosine, sine):
    half_width = values_in.shape[-1] // 2
    front_half = values_in[..., :half_width]
    back_half = values_in[..., half_width:]
    return jnp.concatenate([front_half * cosine - back_half * sine, back_half * cosine + front_half * sine], axis=-1)

def angles(positions):
    half_width = HEAD // 2
    frequency = jnp.power(jnp.float32(1000000.0), jnp.arange(half_width).astype(jnp.float32) * (-2.0 / HEAD))
    angle_rows = positions.astype(jnp.float32)[:, None] * frequency[None, :]
    return (jnp.cos(angle_rows), jnp.sin(angle_rows))

def attend_sequence(query_rot, key_rot, value_rows, seq_positions):
    seq_length = query_rot.shape[0]
    block_rows = 512 if seq_length % 512 == 0 else seq_length
    block_count = seq_length // block_rows

    def one_block(block_args):
        query_block, query_pos = block_args
        scores = jnp.einsum('bhd,kd->hbk', query_block, key_rot, precision=HIGH) * HEAD ** (-0.5)
        scores = low_back(scores)
        allowed = seq_positions[None, None, :] <= query_pos[None, :, None]
        scores = jnp.where(allowed, scores, -1e+30)
        row_top = lax.optimization_barrier(jnp.max(scores, axis=-1, keepdims=True))
        exponent = jnp.exp(scores - row_top)
        probs = low(exponent / lax.optimization_barrier(jnp.sum(exponent, axis=-1, keepdims=True)))
        return jnp.einsum('hbk,kd->bhd', probs, value_rows, precision=HIGH)
    blocks = lax.map(jax.checkpoint(one_block), (query_rot.reshape(block_count, block_rows, HEADS, HEAD), seq_positions.reshape(block_count, block_rows)))
    return blocks.reshape(seq_length, HEADS, HEAD)

def forward(tokens, query_weight, keyvalue_weight, output_weight, gate_weight, up_weight, down_weight, attn_in_gain, attn_out_gain, ffn_in_gain, ffn_out_gain, query_gain, key_gain, cosine, sine, positions):
    normed = low(unit_rows(tokens) * attn_in_gain)
    queries = low_back(jnp.dot(normed, query_weight, precision=HIGH)).reshape(TOKENS, HEADS, HEAD)
    keyvalue = low_back(jnp.dot(normed, keyvalue_weight, precision=HIGH))
    key_rot = low(rotate(unit_rows(keyvalue[:, :HEAD]) * key_gain, cosine, sine))
    value_rows = low(keyvalue[:, HEAD:])
    query_rot = low(rotate(unit_rows(queries) * query_gain, cosine[:, None, :], sine[:, None, :]))
    attended = lax.map(lambda seq_args: attend_sequence(seq_args[0], seq_args[1], seq_args[2], seq_args[3]), (query_rot.reshape(SEQS, LENGTH, HEADS, HEAD), key_rot.reshape(SEQS, LENGTH, HEAD), value_rows.reshape(SEQS, LENGTH, HEAD), positions.reshape(SEQS, LENGTH)))
    mixed_heads = low(low_back(attended.reshape(TOKENS, HEADS * HEAD)))
    attn_branch = low_back(jnp.dot(mixed_heads, output_weight.T, precision=HIGH))
    middle = tokens + unit_rows(attn_branch) * attn_out_gain
    normed_ffn = low(unit_rows(middle) * ffn_in_gain)
    gate_proj = low_back(jnp.dot(normed_ffn, gate_weight, precision=HIGH))
    up_proj = low_back(jnp.dot(normed_ffn, up_weight, precision=HIGH))
    hidden = low(jax.nn.gelu(gate_proj, approximate=True) * up_proj)
    ffn_branch = low_back(jnp.dot(hidden, down_weight.T, precision=HIGH))
    return middle + unit_rows(ffn_branch) * ffn_out_gain

def reference(tokens, query_weight, keyvalue_weight, output_weight, gate_weight, up_weight, down_weight, attn_in_gain, attn_out_gain, ffn_in_gain, ffn_out_gain, query_gain, key_gain, positions, cotangent):
    floats = [arr.astype(jnp.float32) for arr in (tokens, query_weight, keyvalue_weight, output_weight, gate_weight, up_weight, down_weight, attn_in_gain, attn_out_gain, ffn_in_gain, ffn_out_gain, query_gain, key_gain)]
    cosine, sine = angles(positions)
    result, pullback = jax.vjp(lambda *params: forward(*params, cosine, sine, positions), *floats)
    grads = pullback(cotangent.astype(jnp.float32))
    return (result.astype(jnp.bfloat16), grads[0], grads[1], grads[2], grads[3], grads[4], grads[5], grads[6], grads[7], grads[8], grads[9], grads[10], grads[11], grads[12])
```

```python
import jax
import jax.numpy as jnp
from jax import lax
from jax.sharding import PartitionSpec as P

EPS = 1e-06
BF = jnp.bfloat16
F32 = jnp.float32
ROWS = ("shard", "context")


def inv_rms(values_in):
    return lax.rsqrt(jnp.mean(values_in * values_in, axis=-1, keepdims=True) + EPS)


def rms_back(normal, factor, incoming):
    return factor * (incoming - normal * jnp.mean(incoming * normal, axis=-1, keepdims=True))


def rotate(values_in, cosine, sine):
    half_width = values_in.shape[-1] // 2
    front_half = values_in[..., :half_width]
    back_half = values_in[..., half_width:]
    return jnp.concatenate(
        [front_half * cosine - back_half * sine, back_half * cosine + front_half * sine], axis=-1
    )


def angles(positions, head_width):
    half_width = head_width // 2
    frequency = jnp.power(
        jnp.float32(1000000.0), jnp.arange(half_width).astype(jnp.float32) * (-2.0 / head_width)
    )
    angle_rows = positions.astype(jnp.float32)[:, None] * frequency[None, :]
    return (jnp.cos(angle_rows), jnp.sin(angle_rows))


def dot_nn(left, right):
    return jnp.dot(left, right, preferred_element_type=F32)


def dot_nt(left, right):
    return lax.dot_general(left, right, (((1,), (1,)), ((), ())), preferred_element_type=F32)


def dot_tn(left, right):
    return lax.dot_general(left, right, (((0,), (0,)), ((), ())), preferred_element_type=F32)


def exchange(x, axis, size, flip):
    return lax.ppermute(x, axis, [(i, i ^ flip) for i in range(size)])


class Chips:
    def __init__(self, mesh_shape, width):
        self.n_c, self.n_t = mesh_shape["context"], mesh_shape["tensor"]
        self.s, self.c, self.z = (lax.axis_index(a) for a in ("shard", "context", "tensor"))
        self.block = width // 8
        local = jnp.arange(width, dtype=jnp.int32)
        blk = local // self.block
        true_blk = (self.s ^ (blk // 2)) * 2 + ((blk % 2) ^ (self.z // 2))
        self.true_blk = true_blk[:: self.block]
        true_col = true_blk * self.block + local % self.block
        self.place = (jnp.arange(width, dtype=jnp.int32)[:, None] == true_col[None, :]).astype(BF)

    def to_local(self, x):
        return dot_nn(x, self.place).astype(x.dtype)

    def to_local_f32(self, x):
        return jnp.dot(x, self.place.astype(F32), precision=lax.Precision.HIGHEST)

    def to_true(self, x):
        return dot_nt(x, self.place).astype(x.dtype)

    def blocks_to_local(self, x):
        pick = (jnp.arange(8)[None, :] == self.true_blk[:, None]).astype(F32)
        return jnp.dot(pick, x, precision=lax.Precision.HIGHEST)

    def _plane_perm(self, k1, k0):
        perm = []
        for d in range(2):
            for z in range(4):
                src = (k1 ^ (z >> 1)) * 4 + 2 * d + ((z & 1) ^ k0)
                perm.append((src, d * 4 + z))
        return perm

    def pieces_in(self, x):
        return [
            jnp.concatenate(
                [lax.ppermute(x, ("context", "tensor"), self._plane_perm(k1, k0)) for k1 in range(2)], axis=0
            )
            for k0 in range(2)
        ]

    def pieces_out(self, pair):
        total = None
        for k1 in range(2):
            for k0 in range(2):
                piece = pair[k0][k1 * self.block : (k1 + 1) * self.block].astype(BF)
                perm = [(b, a) for a, b in self._plane_perm(k1, k0)]
                got = lax.ppermute(piece, ("context", "tensor"), perm).astype(F32)
                total = got if total is None else total + got
        return total

    def rows_in(self, a, b):
        n = a.shape[0]
        ax, by = exchange(a, "shard", 4, 1), exchange(b, "shard", 4, 2)
        a2, b2 = jnp.concatenate([a, ax], axis=0), jnp.concatenate([b, by], axis=0)
        ay, bx = exchange(a2, "shard", 4, 2), exchange(b2, "shard", 4, 1)
        return (
            jnp.concatenate([a2, ay], axis=0),
            jnp.concatenate([b, bx[:n], by, bx[n:]], axis=0),
        )

    def rows_out(self, a, b):
        n = a.shape[0] // 4
        ga = exchange(jnp.concatenate([a[n : 2 * n], a[3 * n :]], axis=0).astype(BF), "shard", 4, 1).astype(F32)
        gb = exchange(b[2 * n :].astype(BF), "shard", 4, 2).astype(F32)
        a_far = (a[2 * n : 3 * n].astype(F32) + ga[n:]).astype(BF)
        b_far = (b[n : 2 * n].astype(F32) + gb[n:]).astype(BF)
        ha, hb = exchange(a_far, "shard", 4, 2).astype(F32), exchange(b_far, "shard", 4, 1).astype(F32)
        return a[:n].astype(F32) + ga[:n] + ha, b[:n].astype(F32) + gb[:n] + hb

    def gather_pair(self, x):
        return self.rows_in(*self.pieces_in(x))

    def scatter_pair(self, a, b):
        return self.pieces_out(self.rows_out(a, b))

    def gather_shared(self, x):
        half = x.shape[1] // 2
        mine = lax.dynamic_slice_in_dim(x, self.c * half, half, axis=1)
        theirs = lax.dynamic_slice_in_dim(x, (1 - self.c) * half, half, axis=1)
        got = exchange(theirs, "context", 2, 1)
        first = self.c == self.z // 2
        rows = jnp.concatenate([jnp.where(first, mine, got), jnp.where(first, got, mine)], axis=0)
        quarter = half // 2
        a, b = self.rows_in(rows[:, :quarter], rows[:, quarter:])
        whole = jnp.concatenate([a, b], axis=1)
        other = exchange(whole, "context", 2, 1)
        low = self.c == 0
        return jnp.concatenate([jnp.where(low, whole, other), jnp.where(low, other, whole)], axis=1)

    def scatter_shared(self, x):
        cols = x.shape[1]
        split = x.astype(BF).reshape(4, 2, self.block, cols)
        k1 = self.c ^ (self.z // 2)
        mine = lax.dynamic_index_in_dim(split, k1, axis=1, keepdims=False)
        theirs = lax.dynamic_index_in_dim(split, 1 - k1, axis=1, keepdims=False)
        total = mine.astype(F32) + exchange(theirs, "context", 2, 1).astype(F32)
        sends = total.astype(BF)
        block_sum = total[0]
        for k in (1, 2, 3):
            block_sum = block_sum + exchange(sends[k], "shard", 4, k).astype(F32)
        low = block_sum.astype(BF)
        got = [low.astype(F32)] + [exchange(low, "tensor", 4, k).astype(F32) for k in (1, 2, 3)]
        return (got[0] + got[1]) + (got[2] + got[3])

    def tokens_out(self, x):
        n = x.shape[0]
        out = jnp.zeros((4 * n, x.shape[1]), x.dtype)
        for k in range(4):
            piece = x if k == 0 else exchange(x, "tensor", 4, k)
            out = lax.dynamic_update_slice_in_dim(out, piece, (self.z ^ k) * n, axis=0)
        return out

    def keys_all(self, x):
        return jnp.concatenate([x, exchange(x, "context", 2, 1)], axis=0)

    def keys_back(self, x):
        half = x.shape[0] // 2
        total = x[:half].astype(F32) + exchange(x[half:].astype(BF), "context", 2, 1).astype(F32)
        low = total.astype(BF)
        n = half // 4
        own = lax.dynamic_slice_in_dim(total, self.z * n, n, axis=0)
        for k in (1, 2, 3):
            piece = lax.dynamic_slice_in_dim(low, (self.z ^ k) * n, n, axis=0)
            own = own + exchange(piece, "tensor", 4, k).astype(F32)
        return own


class Slice:
    def __init__(self, mesh_shape, width):
        self.n_s, self.n_c, self.n_t = (mesh_shape[a] for a in ("shard", "context", "tensor"))
        self.s, self.c, self.z = (lax.axis_index(a) for a in ("shard", "context", "tensor"))
        self.core = self.c % 2

    def to_local(self, x):
        return x

    to_local_f32 = to_true = blocks_to_local = to_local

    def gather_pair(self, x):
        whole = lax.all_gather(lax.all_gather(x, ROWS, axis=0, tiled=True), "tensor", axis=0)
        return tuple(
            lax.dynamic_index_in_dim(whole, 2 * self.core + j, axis=0, keepdims=False) for j in range(2)
        )

    def scatter_pair(self, a, b):
        out = jnp.zeros((self.n_t,) + a.shape, F32)
        out = lax.dynamic_update_slice_in_dim(
            out, jnp.stack([a, b]).astype(F32), 2 * self.core, axis=0
        )
        out = lax.psum_scatter(out, "tensor", scatter_dimension=0, tiled=False)
        return lax.psum_scatter(out, ROWS, scatter_dimension=0, tiled=True)

    def gather_shared(self, x):
        return lax.all_gather(x, ROWS, axis=0, tiled=True)

    def scatter_shared(self, x):
        return lax.psum(lax.psum_scatter(x, ROWS, scatter_dimension=0, tiled=True), "tensor")

    def tokens_out(self, x):
        return lax.all_gather(x, "tensor", axis=0, tiled=True)

    def keys_all(self, x):
        return lax.all_gather(x, "context", axis=0, tiled=True)

    def keys_back(self, x):
        part = lax.psum_scatter(x, "context", scatter_dimension=0, tiled=True)
        return lax.psum_scatter(part, "tensor", scatter_dimension=0, tiled=True)


def layer(
    mesh_shape,
    tokens,
    query_weight,
    keyvalue_weight,
    output_weight,
    gate_weight,
    up_weight,
    down_weight,
    attn_in_gain,
    attn_out_gain,
    ffn_in_gain,
    ffn_out_gain,
    query_gain,
    key_gain,
    positions,
    cotangent,
):
    width = tokens.shape[1]
    n_s, n_c, n_t = (mesh_shape[a] for a in ("shard", "context", "tensor"))
    move = (Chips if (n_s, n_c, n_t) == (4, 2, 4) else Slice)(mesh_shape, width)
    z = lax.axis_index("tensor")
    core = lax.axis_index("context") % 2
    low_core = core == 0
    swap = lambda x: exchange(x, "context", n_c, 1)
    head = query_weight.shape[1]
    hid = gate_weight.shape[1]
    scale = head ** (-0.5)
    row_count = tokens.shape[0]
    part = row_count // n_t
    own_rows = lambda x: lax.dynamic_slice_in_dim(x, core * part, part, axis=0)
    other_rows = lambda x: lax.dynamic_slice_in_dim(x, (1 - core) * part, part, axis=0)
    in_order = lambda own, other: jnp.concatenate(
        [jnp.where(low_core, own, other), jnp.where(low_core, other, own)], axis=0
    )

    kv_w = move.gather_shared(keyvalue_weight)
    q_w = move.gather_pair(query_weight)
    gup_w = move.gather_pair(jnp.concatenate([output_weight, gate_weight, up_weight], axis=1))
    o_w = [w[:, :head] for w in gup_w]
    gu_w = [w[:, head:] for w in gup_w]
    d_w = move.gather_pair(down_weight)

    slot = lambda x: lax.dynamic_slice_in_dim(x, z * part, part, axis=0)
    own_pack = jnp.concatenate([slot(tokens), slot(cotangent)], axis=0)
    other_pack = swap(own_pack)
    other_pos = swap(positions)
    chip_pack = move.to_local(
        jnp.concatenate(
            [in_order(own_pack[:part], other_pack[:part]), in_order(own_pack[part:], other_pack[part:])]
        )
    )
    inputs = chip_pack[: 2 * part].astype(F32)
    upstream = chip_pack[2 * part :].astype(F32)
    gains = move.to_local_f32(jnp.stack([attn_in_gain, attn_out_gain, ffn_in_gain, ffn_out_gain]))
    g_attn_in, g_attn_out, g_ffn_in, g_ffn_out = (gains[i] for i in range(4))

    all_inputs = move.to_local(tokens).astype(F32)
    all_normed = (all_inputs * inv_rms(all_inputs) * g_attn_in).astype(BF)
    cos_k, sin_k = angles(positions, head)
    keyvalue = dot_nn(all_normed, kv_w)
    keys = keyvalue[:, :head]
    key_rot = rotate(keys * inv_rms(keys) * key_gain, cos_k, sin_k).astype(BF)
    kv_pack = jnp.concatenate([key_rot, keyvalue[:, head:].astype(BF)], axis=1)
    kv_all = move.keys_all(kv_pack)
    all_keys, all_values = kv_all[:, :head], kv_all[:, head:]
    if n_c == 2:
        key_pos = jnp.concatenate([positions, other_pos])
    else:
        key_pos = lax.all_gather(positions, "context", axis=0, tiled=True)
    own_keys = slot(keys)

    unit_in_factor = inv_rms(inputs)
    unit_in = inputs * unit_in_factor
    normed = (unit_in * g_attn_in).astype(BF)
    query_pos = in_order(slot(positions), slot(other_pos))
    cos_o, sin_o = angles(slot(other_pos), head)
    cos_s, sin_s = slot(cos_k), slot(sin_k)
    cos_q, sin_q = in_order(cos_s, cos_o), in_order(sin_s, sin_o)
    allowed = key_pos[None, :] <= query_pos[:, None]
    q_unit, q_factor, q_rot, log_totals, mixed = [], [], [], [], []
    for j in range(2):
        proj = dot_nn(normed, q_w[j])
        factor = inv_rms(proj)
        unit = proj * factor
        rot = rotate(unit * query_gain, cos_q, sin_q).astype(BF)
        scores = jnp.where(allowed, dot_nt(rot, all_keys) * scale, -1e30)
        row_top = jnp.max(scores, axis=-1, keepdims=True)
        exponent = jnp.exp(scores - row_top)
        normalizer = jnp.sum(exponent, axis=-1, keepdims=True)
        probs_low = (exponent / normalizer).astype(BF)
        mixed.append(dot_nn(probs_low, all_values).astype(BF))
        q_unit.append(unit)
        q_factor.append(factor)
        q_rot.append(rot)
        log_totals.append(row_top + jnp.log(normalizer))

    def chip_sum(x):
        low = x.astype(BF)
        return low.astype(F32) + swap(low).astype(F32)

    attn_branch = chip_sum(dot_nt(mixed[0], o_w[0]) + dot_nt(mixed[1], o_w[1]))
    attn_factor = inv_rms(attn_branch)
    unit_attn = attn_branch * attn_factor
    middle = inputs + unit_attn * g_attn_out
    mid_factor = inv_rms(middle)
    unit_mid = middle * mid_factor
    normed_ffn = (unit_mid * g_ffn_in).astype(BF)

    hidden, act_up, pulls = [], [], []
    for j in range(2):
        both = dot_nn(normed_ffn, gu_w[j])
        gate, up = both[:, :hid], both[:, hid:]
        activated, pull = jax.vjp(lambda gate_in: jax.nn.gelu(gate_in, approximate=True), gate)
        hidden.append((activated * up).astype(BF))
        act_up.append((activated, up))
        pulls.append(pull)
    ffn_branch = chip_sum(dot_nt(hidden[0], d_w[0]) + dot_nt(hidden[1], d_w[1]))
    ffn_factor = inv_rms(ffn_branch)
    unit_ffn = ffn_branch * ffn_factor
    mixed_own = own_rows((middle + unit_ffn * g_ffn_out).astype(BF))
    mixed_out = move.tokens_out(move.to_true(mixed_own))

    ffn_out_grad = jnp.sum(upstream * unit_ffn, axis=0) * 0.5
    branch_grad = rms_back(unit_ffn, ffn_factor, upstream * g_ffn_out).astype(BF)
    ffn_normed_grad = 0.0
    grads = []
    for j in range(2):
        activated, up = act_up[j]
        hidden_grad = dot_nn(branch_grad, d_w[j])
        gate_rows = pulls[j](hidden_grad * up)[0].astype(BF)
        up_rows = (hidden_grad * activated).astype(BF)
        rows = jnp.concatenate([gate_rows, up_rows], axis=1)
        ffn_normed_grad = ffn_normed_grad + dot_nt(rows, gu_w[j])
        grads.append(
            jnp.concatenate(
                [dot_tn(normed_ffn, rows).astype(BF), dot_tn(branch_grad, hidden[j]).astype(BF)], axis=1
            )
        )
    ffn_normed_grad = chip_sum(ffn_normed_grad)
    ffn_in_grad = jnp.sum(ffn_normed_grad * unit_mid, axis=0) * 0.5
    middle_grad = upstream + rms_back(unit_mid, mid_factor, ffn_normed_grad * g_ffn_in)
    attn_out_grad = jnp.sum(middle_grad * unit_attn, axis=0) * 0.5
    attn_rows = rms_back(unit_attn, attn_factor, middle_grad * g_attn_out).astype(BF)
    o_grads = [dot_tn(attn_rows, mixed[j]).astype(BF) for j in range(2)]
    ffn_scattered = move.scatter_pair(
        *[jnp.concatenate([grads[j], o_grads[j]], axis=1) for j in range(2)]
    )
    gate_grad = ffn_scattered[:, :hid]
    up_grad = ffn_scattered[:, hid : 2 * hid]
    down_grad = ffn_scattered[:, 2 * hid : 3 * hid]
    output_grad = ffn_scattered[:, 3 * hid :]

    key_acc = 0.0
    value_acc = 0.0
    normed_part = 0.0
    q_grads = []
    query_gain_sum = 0.0
    for j in range(2):
        head_rows = dot_nn(attn_rows, o_w[j]).astype(BF)
        scores = jnp.where(allowed, dot_nt(q_rot[j], all_keys) * scale, -1e30)
        probs = jnp.exp(scores - log_totals[j])
        prob_grad = dot_nt(head_rows, all_values)
        centre = jnp.sum(probs * prob_grad, axis=-1, keepdims=True)
        score_grad = (probs * (prob_grad - centre)).astype(BF)
        query_rot_grad = dot_nn(score_grad, all_keys) * scale
        key_acc = key_acc + dot_tn(score_grad, q_rot[j]) * scale
        value_acc = value_acc + dot_tn(probs.astype(BF), head_rows)
        query_normed = rotate(query_rot_grad, cos_q, -sin_q)
        query_gain_sum = query_gain_sum + jnp.sum(query_normed * q_unit[j], axis=0)
        query_rows = rms_back(q_unit[j], q_factor[j], query_normed * query_gain).astype(BF)
        q_grads.append(dot_tn(normed, query_rows).astype(BF))
        normed_part = normed_part + dot_nt(query_rows, q_w[j])
    query_grad = move.scatter_pair(*q_grads)

    kv_grad_own = move.keys_back(jnp.concatenate([key_acc, value_acc], axis=1))
    key_normed = rotate(kv_grad_own[:, :head], cos_s, -sin_s)
    key_factor = inv_rms(own_keys)
    key_unit = own_keys * key_factor
    key_gain_sum = jnp.sum(key_normed * key_unit, axis=0)
    keyvalue_rows = jnp.concatenate(
        [rms_back(key_unit, key_factor, key_normed * key_gain), kv_grad_own[:, head:]], axis=1
    ).astype(BF)
    kv_partial = dot_tn(own_rows(normed), keyvalue_rows)

    normed_grad = (
        own_rows(normed_part)
        + swap(other_rows(normed_part).astype(BF)).astype(F32)
        + dot_nt(keyvalue_rows, kv_w)
    )
    own_unit = own_rows(unit_in)
    attn_in_grad = jnp.sum(normed_grad * own_unit, axis=0)
    input_grad_own = own_rows(middle_grad) + rms_back(
        own_unit, own_rows(unit_in_factor), normed_grad * g_attn_in
    )
    input_grad = move.tokens_out(move.to_true(input_grad_own.astype(BF))).astype(F32)

    blocks = n_s * n_c
    block_rows = width // blocks
    head_rows_out = head // blocks
    small = jnp.concatenate(
        [move.blocks_to_local(v.reshape(blocks, head_rows_out)) for v in (query_gain_sum, key_gain_sum)],
        axis=0,
    ).reshape(2, blocks, head_rows_out)
    small = jnp.pad(small, ((0, 0), (0, 0), (0, block_rows - head_rows_out))).reshape(2, width)
    vectors = jnp.concatenate(
        [
            jnp.stack([attn_in_grad, attn_out_grad, ffn_in_grad, ffn_out_grad]),
            small,
            jnp.zeros((122, width), F32),
        ],
        axis=0,
    )
    last = move.scatter_shared(jnp.concatenate([kv_partial, vectors.T], axis=1))
    keyvalue_grad = last[:, : 2 * head]
    ends = [last[:, 2 * head + i] for i in range(6)]
    return (
        mixed_out,
        input_grad,
        query_grad,
        keyvalue_grad,
        output_grad,
        gate_grad,
        up_grad,
        down_grad,
        ends[0],
        ends[1],
        ends[2],
        ends[3],
        ends[4][:head_rows_out],
        ends[5][:head_rows_out],
    )


def solution(mesh):
    rows = P(ROWS)
    grid = P(ROWS, "tensor")
    in_specs = (rows, grid, rows, grid, grid, grid, grid) + (P(),) * 6 + (rows, rows)
    out_specs = (rows, rows, grid, rows, grid, grid, grid, grid) + (rows,) * 6
    shape = {name: mesh.shape[name] for name in mesh.axis_names}

    def body(*args):
        return layer(shape, *args)

    return jax.shard_map(body, mesh=mesh, in_specs=in_specs, out_specs=out_specs, check_vma=False)
```
